32 devices in a mesh: seq: 8 (over y, x, core), rep: 4 (over z).
Axes of the slice: x: 2, y: 2, z: 4, core: 2. Of those that a mesh axis runs over, the one named last changes fastest.
Arguments:
- histories: bfloat16 [4, 8, 6, 64, 512], P('rep', 'seq'), may hold values from -6 to 6
- cotangents: bfloat16 [4, 8, 6, 64, 512], P('rep', 'seq'), may hold values from -6 to 6
- lengths: int32 [4, 8, 6], P('rep', 'seq'), may hold values from 0 to 64, as said below
- w_in: bfloat16 [512, 2048], replicated, may hold values from -0.25 to 0.25
- w_out: bfloat16 [512, 512], replicated, may hold values from -0.25 to 0.25
Outputs:
- input_grads: bfloat16 [4, 8, 6, 64, 512], P('rep', 'seq')
- w_in_grad: float32 [512, 2048], P('rep', 'seq')
The draws below stay inside these ranges and needn't reach their ends.
Inputs may be any that keep to these rules, and one draw needn't show every extreme that they name: `lengths`: in each replica group exactly 16 slots have a positive length, every live length is at least 8, and in each group some rank has all 6 of its slots live.
All inputs are finite; a program needn't handle non-finite values.
Results may differ from the reference program's by a relative error of at most 0.025.
Values may be sent and summed in bfloat16 or wider, within the bound.
A program may use at most 64 MiB of HBM per device.

```python
import jax
import jax.numpy as jnp
from jax import lax

D = 512
HEADS = 8
MAXLEN = 64
HOME = 6
CAP = 2
REPLICAS = 4
RANKS = 8
N_SEQ = 8
N_REP = 4


def draw_lengths(key, part):

    def one_group(group_key):
        slot_total = RANKS * HOME
        keys_list = jax.random.split(group_key, 4)
        shuffled = jax.random.permutation(keys_list[0], slot_total).astype(jnp.int32)
        heavy_rank = jax.random.randint(keys_list[1], (), 0, RANKS)
        slot_index = jnp.arange(slot_total, dtype=jnp.int32)
        ranking = shuffled - jnp.where(slot_index // HOME == heavy_rank, slot_total, 0)
        ordered = jnp.argsort(ranking)
        is_live = jnp.zeros(slot_total, jnp.int32).at[ordered[:CAP * RANKS]].set(1)
        lowest = MAXLEN // 8
        first_draw = jax.random.randint(keys_list[2], (slot_total,), 0, MAXLEN - lowest + 1)
        second_draw = jax.random.randint(keys_list[3], (slot_total,), 0, MAXLEN - lowest + 1)
        sizes = MAXLEN - first_draw * second_draw // (MAXLEN - lowest)
        return (sizes * is_live).astype(jnp.int32).reshape(RANKS, HOME)
    group_keys = jax.random.split(jax.random.fold_in(key, 11), REPLICAS)
    return jax.vmap(one_group)(group_keys)


def block_levels(stream_key, dims, cuts, low, largest):
    level = 1.0
    for axis_at, blocks in cuts:
        heights = jax.random.uniform(jax.random.fold_in(jax.random.fold_in(stream_key, 6), axis_at), (blocks,), jnp.float32, low / len(cuts), largest / len(cuts))
        level = level * jnp.repeat(jnp.exp(heights), dims[axis_at] // blocks).reshape((-1,) + (1,) * (len(dims) - 1 - axis_at))
    return level


def centred(own_key, dims, scale, reach, cuts=(), kind=jnp.bfloat16):
    result = scale * jax.random.normal(own_key, dims, jnp.float32)
    if cuts:
        result = result * block_levels(own_key, dims, cuts, -0.22, 0.18)
    return jnp.clip(result, -reach, reach).astype(kind)


def setup_inputs(seed: int = 0) -> dict:
    streams_of = jax.random.split(jax.random.key(seed), 6)
    return {
        "histories": centred(streams_of[0], (REPLICAS, RANKS, HOME, MAXLEN, D), 1.0, 6.0, ((0, 4), (1, 8))),
        "cotangents": centred(streams_of[1], (REPLICAS, RANKS, HOME, MAXLEN, D), 1.0, 6.0, ((0, 4), (1, 8))),
        "lengths": draw_lengths(jax.random.fold_in(streams_of[5], 71), 0),
        "w_in": centred(streams_of[3], (D, 4 * D), D ** -0.5, 0.25),
        "w_out": centred(streams_of[4], (D, D), D ** -0.5, 0.25),
    }


def layer_norm(values):
    average = lax.optimization_barrier(jnp.mean(values, axis=-1, keepdims=True))
    centered = values - average
    spread = lax.optimization_barrier(jnp.mean(centered * centered, axis=-1, keepdims=True))
    return centered * lax.rsqrt(spread + 1e-06)

def forward(history, weight_in, weight_out, lengths):
    count_slots, positions, features = history.shape
    head_size = features // HEADS
    normed = layer_norm(history.astype(jnp.float32)).astype(jnp.bfloat16)
    projected = jax.nn.silu(jnp.dot(normed.reshape(count_slots * positions, features), weight_in, preferred_element_type=jnp.float32)).astype(jnp.bfloat16)
    projected = projected.reshape(count_slots, positions, 4, HEADS, head_size)
    gate_rows = projected[:, :, 0].reshape(count_slots, positions, features)
    value_rows = projected[:, :, 1]
    query_rows = projected[:, :, 2]
    key_rows = projected[:, :, 3]
    scores = jnp.einsum('cthe,cshe->chts', query_rows, key_rows, preferred_element_type=jnp.float32) * head_size ** (-0.5)
    row_ids = jnp.arange(positions, dtype=jnp.int32)
    allowed = (row_ids[None, :] <= row_ids[:, None])[None, None] & (row_ids[None, None, None, :] < lengths[:, None, None, None])
    weights = (jnp.where(allowed, jax.nn.silu(scores), 0.0) / lengths.astype(jnp.float32)[:, None, None, None]).astype(jnp.bfloat16)
    attended = jnp.einsum('chts,cshe->cthe', weights, value_rows, preferred_element_type=jnp.float32).reshape(count_slots, positions, features)
    gated_out = (layer_norm(attended) * gate_rows.astype(jnp.float32)).astype(jnp.bfloat16)
    mixed_out = jnp.dot(gated_out.reshape(count_slots * positions, features), weight_out, preferred_element_type=jnp.float32)
    return history.astype(jnp.float32) + mixed_out.reshape(count_slots, positions, features)

def cotangent_seed(cotangent, lengths):
    row_ids = jnp.arange(cotangent.shape[1], dtype=jnp.int32)
    valid = row_ids[None, :] < lengths[:, None]
    return jnp.where(valid[:, :, None], cotangent.astype(jnp.float32), 0.0)

def assign(flat_lengths, devices, home_slots):
    slot_total = devices * home_slots
    slot_index = jnp.arange(slot_total, dtype=jnp.int32)
    is_live = flat_lengths > 0
    work_cost = flat_lengths * flat_lengths
    ranking = jnp.where(is_live, slot_index - work_cost * slot_total, slot_total * slot_total + slot_index)
    ordered = jnp.argsort(ranking).astype(jnp.int32)
    leading = ordered[:devices]
    trailing = ordered[devices:2 * devices][::-1]
    device_ids = jnp.arange(devices, dtype=jnp.int32)
    partner_ids = trailing[(device_ids[None, :] + device_ids[:, None]) % devices]
    clashes = jnp.any(leading[None, :] // home_slots == partner_ids // home_slots, axis=1)
    chosen_shift = jnp.argmin(jnp.where(clashes, devices + device_ids, device_ids)).astype(jnp.int32)
    usable = jnp.logical_not(jnp.all(clashes))
    partners = trailing[(device_ids + chosen_shift) % devices]
    paired_dest = jnp.zeros(slot_total, jnp.int32).at[leading].set(device_ids).at[partners].set(device_ids)
    paired_slot = jnp.zeros(slot_total, jnp.int32).at[partners].set(1)
    position = jnp.cumsum(is_live.astype(jnp.int32)).astype(jnp.int32) - 1
    destination = jnp.where(is_live, jnp.where(usable, paired_dest, position % devices), -1)
    arrival = jnp.where(is_live, jnp.where(usable, paired_slot, position // devices), -1)
    return (destination, arrival)

def reference(histories, cotangents, lengths, w_in, w_out):
    devices = N_SEQ
    groups = N_REP
    slot_total = devices * HOME
    flat_hist = histories.reshape(groups * slot_total, MAXLEN, D)
    flat_cot = cotangents.reshape(groups * slot_total, MAXLEN, D)
    flat_lengths = lengths.reshape(groups, slot_total)
    destination, arrival = jax.vmap(lambda lengths_row: assign(lengths_row, devices, HOME))(flat_lengths)
    slot_index = jnp.arange(slot_total, dtype=jnp.int32)
    selected = (destination[:, None, None, :] == jnp.arange(devices, dtype=jnp.int32)[None, :, None, None]) & (arrival[:, None, None, :] == jnp.arange(CAP, dtype=jnp.int32)[None, None, :, None])
    members = lax.optimization_barrier(jnp.sum(jnp.where(selected, slot_index, 0), axis=3)).astype(jnp.int32)
    group_ids = jnp.repeat(jnp.arange(groups, dtype=jnp.int32), devices)
    members_flat = members.reshape(groups * devices, CAP)
    lengths_all = flat_lengths.reshape(groups * slot_total)

    def one_device(total, item):
        group_id, picked = item
        rows_at = group_id * slot_total + picked
        history = flat_hist[rows_at]
        cotangent = flat_cot[rows_at]
        picked_lengths = lengths_all[rows_at]
        _, pullback = jax.vjp(lambda history_in, weight_in: forward(history_in, weight_in, w_out, picked_lengths), history, w_in)
        grad_hist, grad_in = pullback(cotangent_seed(cotangent, picked_lengths))
        return (total + grad_in.astype(jnp.float32), grad_hist)
    total, grads = lax.scan(one_device, jnp.zeros((D, 4 * D), jnp.float32), (group_ids, members_flat))
    home_index = jnp.arange(groups, dtype=jnp.int32)[:, None] * (devices * CAP) + destination * CAP + arrival
    home = grads.reshape(groups * devices * CAP, MAXLEN, D)[jnp.clip(home_index, 0, groups * devices * CAP - 1)]
    home = jnp.where((flat_lengths > 0)[:, :, None, None], home, jnp.zeros((), home.dtype)).astype(jnp.bfloat16)
    return (home.reshape(histories.shape), total)
```

```python
import functools

import jax
import jax.numpy as jnp
from jax import lax
from jax.experimental import pallas as pl
from jax.experimental.pallas import tpu as pltpu
from jax.sharding import PartitionSpec as P

HEADS = 8
GROUP = 4
CHUNKS = 2
MESH = pl.DeviceIdType.MESH
F32 = jnp.float32
BF16 = jnp.bfloat16


def dot(left, right, left_dim, right_dim):
    return lax.dot_general(
        left, right, (((left_dim,), (right_dim,)), ((), ())), preferred_element_type=F32
    )


def norm_parts(values):
    average = jnp.mean(values, axis=-1, keepdims=True)
    centered = values - average
    spread = jnp.mean(centered * centered, axis=-1, keepdims=True)
    scale = lax.rsqrt(spread + 1e-06)
    return centered * scale, scale


def norm_back(normed, scale, cotangent):
    average = jnp.mean(cotangent, axis=-1, keepdims=True)
    along = jnp.mean(cotangent * normed, axis=-1, keepdims=True)
    return scale * (cotangent - average - normed * along)


def local_body(slots, positions, features, lens_ref, hist_hbm, cot_hbm, win_hbm, wout_hbm,
               emit, finish, hist, cot, win, wout, normed, normed_t, proj, slope, dgate,
               dproj, sems):
    rows = slots * positions
    head = features // HEADS
    width = GROUP * head
    quads = HEADS // GROUP
    block = 256
    copies = [
        pltpu.make_async_copy(hist_hbm, hist, sems.at[0]),
        pltpu.make_async_copy(win_hbm, win, sems.at[1]),
        pltpu.make_async_copy(cot_hbm, cot, sems.at[2]),
        pltpu.make_async_copy(wout_hbm, wout, sems.at[3]),
    ]
    for copy in copies:
        copy.start()
    row_ids = lax.broadcasted_iota(jnp.int32, (positions, 1), 0)
    copies[0].wait()
    scales = []
    for slot in range(slots):
        part, scale = norm_parts(hist[slot].astype(F32))
        scales.append(scale)
        normed[slot * positions:(slot + 1) * positions, :] = part.astype(BF16)
    copies[1].wait()

    @pl.loop(0, 4 * features // block)
    def _(step):
        columns = pl.ds(pl.multiple_of(step * block, block), block)
        out = dot(normed[...], win[:, columns], 1, 0)
        gate = jax.nn.sigmoid(out)
        proj[:, columns] = (out * gate).astype(BF16)
        slope[:, columns] = gate * (1.0 + out * (1.0 - gate))

    copies[2].wait()
    for slot in range(slots):
        valid = row_ids < lens_ref[0, 0, slot]
        cot[slot] = jnp.where(valid, cot[slot], jnp.zeros((), BF16))
    copies[3].wait()
    dgate[...] = dot(cot[...].reshape(rows, features), wout[...], 1, 1).astype(BF16)

    time_ids = lax.broadcasted_iota(jnp.int32, (positions, width), 0)
    key_ids = lax.broadcasted_iota(jnp.int32, (positions, width), 1) % positions
    causal = key_ids <= time_ids
    lane_head = lax.broadcasted_iota(jnp.int32, (positions, width), 1) // head

    def spread_heads(values):
        zero = jnp.zeros((), values.dtype)
        return jnp.concatenate(
            [jnp.where(lane_head == h, values, zero) for h in range(GROUP)], axis=0
        )

    def gather_heads(values):
        total = values[0:positions]
        for h in range(1, GROUP):
            total = jnp.where(lane_head == h, values[h * positions:(h + 1) * positions], total)
        return total

    def columns_of(kind, quad):
        return slice(kind * features + quad * width, kind * features + (quad + 1) * width)

    for slot in range(slots):
        at = slice(slot * positions, (slot + 1) * positions)
        length = lens_ref[0, 0, slot]
        allowed = causal & (key_ids < length)
        per_length = 1.0 / jnp.full((1, width), jnp.maximum(length, 1), jnp.int32).astype(F32)
        weight_of, slope_of, query_of, keys_of, values_of, attended = [], [], [], [], [], []
        for quad in range(quads):
            query = proj[at, columns_of(2, quad)]
            keys = spread_heads(proj[at, columns_of(3, quad)])
            values = spread_heads(proj[at, columns_of(1, quad)])
            scores = dot(query, keys, 1, 1) * head ** (-0.5)
            gate = jax.nn.sigmoid(scores)
            weights = (jnp.where(allowed, scores * gate, 0.0) * per_length).astype(BF16)
            grade = jnp.where(allowed, gate * (1.0 + scores * (1.0 - gate)), 0.0)
            attended.append(dot(weights, values, 1, 0))
            weight_of.append(weights)
            slope_of.append(grade * (per_length * head ** (-0.5)))
            query_of.append(query)
            keys_of.append(keys)
            values_of.append(values)
        normal, scale = norm_parts(jnp.concatenate(attended, axis=1))
        grad = dgate[at, :].astype(F32)
        gates = proj[at, 0:features].astype(F32)
        dproj[at, 0:features] = (
            (grad * normal).astype(BF16).astype(F32) * slope[at, 0:features]
        ).astype(BF16)
        d_att = norm_back(normal, scale, grad * gates).astype(BF16)
        for quad in range(quads):
            d_quad = d_att[:, quad * width:(quad + 1) * width]
            d_values = gather_heads(dot(weight_of[quad], d_quad, 0, 0))
            d_weights = dot(d_quad, values_of[quad], 1, 1).astype(BF16).astype(F32)
            d_scores = (d_weights * slope_of[quad]).astype(BF16)
            d_query = dot(d_scores, keys_of[quad], 1, 0)
            d_keys = gather_heads(dot(d_scores, query_of[quad], 0, 0))
            for kind, value in ((1, d_values), (2, d_query), (3, d_keys)):
                columns = columns_of(kind, quad)
                dproj[at, columns] = (
                    value.astype(BF16).astype(F32) * slope[at, columns]
                ).astype(BF16)

    normed_t[...] = normed[...].T
    emit(normed_t, dproj)
    for half in range(features // block):
        columns = slice(half * block, (half + 1) * block)
        dgate[:, columns] = dot(dproj[...], win[columns, :], 1, 1).astype(BF16)
    for slot in range(slots):
        at = slice(slot * positions, (slot + 1) * positions)
        grad = norm_back(*norm_parts(hist[slot].astype(F32)), dgate[at, :].astype(F32))
        finish(slot, (cot[slot].astype(F32) + grad).astype(BF16))


def local_scratch(slots, positions, features):
    rows = slots * positions
    return [
        pltpu.VMEM((slots, positions, features), BF16),
        pltpu.VMEM((slots, positions, features), BF16),
        pltpu.VMEM((features, 4 * features), BF16),
        pltpu.VMEM((features, features), BF16),
        pltpu.VMEM((rows, features), BF16),
        pltpu.VMEM((features, rows), BF16),
        pltpu.VMEM((rows, 4 * features), BF16),
        pltpu.VMEM((rows, 4 * features), F32),
        pltpu.VMEM((rows, features), BF16),
        pltpu.VMEM((rows, 4 * features), BF16),
        pltpu.SemaphoreType.DMA((4,)),
    ]


def local_kernel(slots, positions, features, blocked, lens_ref, hist_hbm, cot_hbm, win_hbm,
                 wout_hbm, grad_ref, part_ref, *scratch):
    def emit(normed_t, dproj):
        if not blocked:
            block = 256
            for step in range(4 * features // block):
                columns = slice(step * block, (step + 1) * block)
                part_ref[:, columns] = dot(normed_t[...], dproj[:, columns], 1, 0).astype(BF16)
            return
        ranks, groups = blocked
        width = 4 * features // ranks
        piece = features // groups // CHUNKS

        @pl.loop(0, ranks)
        def _(rank):
            columns = pl.ds(pl.multiple_of(rank * width, width), width)
            total = dot(normed_t[...], dproj[:, columns], 1, 0).astype(BF16)
            for group in range(groups):
                for chunk in range(CHUNKS):
                    start = (group * CHUNKS + chunk) * piece
                    part_ref[chunk, rank, group * piece:(group + 1) * piece, :] = total[
                        start:start + piece
                    ]

    def finish(slot, value):
        grad_ref[0, 0, slot] = value

    local_body(slots, positions, features, lens_ref, hist_hbm.at[0, 0], cot_hbm.at[0, 0],
               win_hbm, wout_hbm, emit, finish, *scratch)


def reduce_kernel(groups, part_ref, out_ref, recv0, acc0, recv1, acc1, recv2, acc2, recv3,
                  s0, r0, s1, r1, s2, r2, s3, r3):
    chunks = part_ref.shape[0]
    piece = part_ref.shape[2] // groups
    me, rep = lax.axis_index("seq"), lax.axis_index("rep")
    core = me % 2
    x_at = (me // 2) % 2
    y_at = me // 4
    a_at = x_at + core * (y_at - x_at)
    b_at = y_at + core * (x_at - y_at)
    a_step, b_step = 1 + core, 2 - core
    twin = me + 1 - 2 * core
    a_peer = me + 2 * a_step * (1 - 2 * a_at)
    b_peer = me + 2 * b_step * (1 - 2 * b_at)
    reps = [(rep + d) % groups for d in range(1, groups)]
    barrier = pltpu.get_barrier_semaphore()
    for peer in (twin, a_peer, b_peer):
        pl.semaphore_signal(barrier, inc=1, device_id={"seq": peer}, device_id_type=MESH)
    for peer in reps:
        pl.semaphore_signal(barrier, inc=1, device_id={"rep": peer}, device_id_type=MESH)
    pl.semaphore_wait(barrier, 3 + len(reps))

    def send(source, target, sent, got, peer):
        copy = pltpu.make_async_remote_copy(
            src_ref=source, dst_ref=target, send_sem=sent, recv_sem=got,
            device_id=peer, device_id_type=MESH,
        )
        copy.start()
        return copy

    def add(left, right):
        return (left.astype(F32) + right.astype(F32)).astype(BF16)

    def chip(a, b):
        return a * a_step + b * b_step

    order = ((1 - a_at, 1 - b_at), (1 - a_at, b_at), (a_at, 1 - b_at), (a_at, b_at))
    first, along, across, last = {}, {}, {}, {}
    for k in range(chunks):
        for i, (a, b) in enumerate(order[j] for j in (0, 2, 1, 3)):
            first[k, i] = send(part_ref.at[k, 2 * chip(a, b) + 1 - core], recv0.at[k, i],
                               s0.at[k, i], r0.at[k, i], {"seq": twin})


    def stage_core(k, i):
        a, b = order[i]
        first[k, i].wait_recv()
        acc0[k, i] = add(part_ref[k, 2 * chip(a, b) + core], recv0[k, i])

    for step in range(chunks + 3):
        k = step
        if k < chunks:
            for i in range(2):
                stage_core(k, i)
                along[k, i] = send(acc0.at[k, i], recv1.at[k, i], s1.at[k, i], r1.at[k, i],
                                   {"seq": a_peer})
            for i in range(2, 4):
                stage_core(k, i)
        k = step - 1
        if 0 <= k < chunks:
            along[k, 0].wait_recv()
            acc1[k, 0] = add(acc0[k, 2], recv1[k, 0])
            across[k] = send(acc1.at[k, 0], recv2.at[k], s2.at[k], r2.at[k], {"seq": b_peer})
            along[k, 1].wait_recv()
            acc1[k, 1] = add(acc0[k, 3], recv1[k, 1])
        k = step - 2
        if 0 <= k < chunks:
            across[k].wait_recv()
            acc2[k] = add(acc1[k, 1], recv2[k])
            for d, peer in enumerate(reps):
                rows = pl.ds(pl.multiple_of(peer * piece, piece), piece)
                last[k, d] = send(acc2.at[k, rows], recv3.at[k, d], s3.at[k, d], r3.at[k, d],
                                  {"rep": peer})
        k = step - 3
        if 0 <= k < chunks:
            rows = pl.ds(pl.multiple_of(rep * piece, piece), piece)
            total = acc2[k, rows].astype(F32)
            for d in range(len(reps)):
                last[k, d].wait_recv()
                total = total + recv3[k, d].astype(F32)
            out_ref[k * piece:(k + 1) * piece, :] = total
    for copies in (first, along, across, last):
        for copy in copies.values():
            copy.wait_send()


def shards(histories, cotangents, lengths, w_in, w_out):
    slots, positions, features = histories.shape[2:]
    ranks, groups = lax.axis_size("seq"), lax.axis_size("rep")
    width = 4 * features // ranks
    tall = features // groups
    fast = ranks == 8 and groups == 4 and width % 128 == 0 and tall % (16 * CHUNKS) == 0
    if fast:
        part_shape = (CHUNKS, ranks, features // CHUNKS, width)
    else:
        part_shape = (features, 4 * features)
    anywhere = pl.BlockSpec(memory_space=pl.ANY)
    inside = pl.BlockSpec(memory_space=pltpu.VMEM)
    grads, part = pl.pallas_call(
        functools.partial(local_kernel, slots, positions, features,
                          (ranks, groups) if fast else None),
        out_shape=(jax.ShapeDtypeStruct(histories.shape, BF16),
                   jax.ShapeDtypeStruct(part_shape, BF16)),
        in_specs=[pl.BlockSpec(memory_space=pltpu.SMEM)] + [anywhere] * 4,
        out_specs=(inside, inside),
        scratch_shapes=local_scratch(slots, positions, features),
        name="local",
    )(lengths, histories, cotangents, w_in, w_out)
    if not fast:
        column_block = lax.psum_scatter(part, "seq", scatter_dimension=1, tiled=True)
        total = lax.psum_scatter(column_block, "rep", scatter_dimension=0, tiled=True)
        return grads, total.astype(F32)
    tile = features // CHUNKS
    shapes = [
        (CHUNKS, 4, tile, width), (CHUNKS, 4, tile, width),
        (CHUNKS, 2, tile, width), (CHUNKS, 2, tile, width),
        (CHUNKS, tile, width), (CHUNKS, tile, width),
        (CHUNKS, groups - 1, tile // groups, width),
    ]
    counts = [(CHUNKS, 4), (CHUNKS, 2), (CHUNKS,), (CHUNKS, groups - 1)]
    total = pl.pallas_call(
        functools.partial(reduce_kernel, groups),
        out_shape=jax.ShapeDtypeStruct((tall, width), F32),
        in_specs=[inside],
        out_specs=inside,
        scratch_shapes=[pltpu.VMEM(shape, BF16) for shape in shapes]
        + [pltpu.SemaphoreType.DMA(count) for count in counts for _ in range(2)],
        compiler_params=pltpu.CompilerParams(collective_id=0, has_side_effects=True),
        name="reduce",
    )(part)
    return grads, total


def solution(mesh):
    placed = (
        P("rep", "seq", None, None, None),
        P("rep", "seq", None, None, None),
        P("rep", "seq", None),
        P(),
        P(),
    )
    return jax.shard_map(
        shards,
        mesh=mesh,
        in_specs=placed,
        out_specs=(P("rep", "seq", None, None, None), P("rep", "seq")),
        check_vma=False,
    )
```

```python
import functools

import jax
import jax.numpy as jnp
from jax import lax
from jax.experimental import pallas as pl
from jax.experimental.pallas import tpu as pltpu
from jax.sharding import PartitionSpec as P

HEADS = 8
GROUP = 4
MESH = pl.DeviceIdType.MESH
F32 = jnp.float32
BF16 = jnp.bfloat16


def dot(left, right, left_dim, right_dim):
    return lax.dot_general(
        left, right, (((left_dim,), (right_dim,)), ((), ())), preferred_element_type=F32
    )


def norm_parts(values):
    average = jnp.mean(values, axis=-1, keepdims=True)
    centered = values - average
    spread = jnp.mean(centered * centered, axis=-1, keepdims=True)
    scale = lax.rsqrt(spread + 1e-06)
    return centered * scale, scale


def norm_back(normed, scale, cotangent):
    average = jnp.mean(cotangent, axis=-1, keepdims=True)
    along = jnp.mean(cotangent * normed, axis=-1, keepdims=True)
    return scale * (cotangent - average - normed * along)


def local_body(slots, positions, features, lens_ref, hist_hbm, cot_hbm, win_hbm, wout_hbm,
               hist, cot, win, wout, normed, normed_t, proj, slope, dgate,
               dproj, kept_weights, kept_grades, sems):
    rows = slots * positions
    head = features // HEADS
    width = GROUP * head
    quads = HEADS // GROUP
    block = 256
    copies = [
        pltpu.make_async_copy(hist_hbm, hist, sems.at[0]),
        pltpu.make_async_copy(win_hbm, win, sems.at[1]),
        pltpu.make_async_copy(cot_hbm, cot, sems.at[2]),
        pltpu.make_async_copy(wout_hbm, wout, sems.at[3]),
    ]
    for copy in copies:
        copy.start()
    row_ids = lax.broadcasted_iota(jnp.int32, (positions, 1), 0)
    copies[0].wait()
    for slot in range(slots):
        part, _ = norm_parts(hist[slot].astype(F32))
        normed[slot * positions:(slot + 1) * positions, :] = part.astype(BF16)
    copies[1].wait()

    @pl.loop(0, 4 * features // block)
    def _(step):
        columns = pl.ds(pl.multiple_of(step * block, block), block)
        out = dot(normed[...], win[:, columns], 1, 0)
        gate = jax.nn.sigmoid(out)
        proj[:, columns] = (out * gate).astype(BF16)
        slope[:, columns] = gate * (1.0 + out * (1.0 - gate))

    copies[2].wait()
    for slot in range(slots):
        valid = row_ids < lens_ref[0, 0, slot]
        cot[slot] = jnp.where(valid, cot[slot], jnp.zeros((), BF16))
    copies[3].wait()
    dgate[...] = dot(cot[...].reshape(rows, features), wout[...], 1, 1).astype(BF16)

    time_ids = lax.broadcasted_iota(jnp.int32, (positions, width), 0)
    key_ids = lax.broadcasted_iota(jnp.int32, (positions, width), 1) % positions
    causal = key_ids <= time_ids
    lane_head = lax.broadcasted_iota(jnp.int32, (positions, width), 1) // head

    def spread_heads(values):
        zero = jnp.zeros((), values.dtype)
        return jnp.concatenate(
            [jnp.where(lane_head == h, values, zero) for h in range(GROUP)], axis=0
        )

    def gather_heads(values):
        total = values[0:positions]
        for h in range(1, GROUP):
            total = jnp.where(lane_head == h, values[h * positions:(h + 1) * positions], total)
        return total

    def columns_of(kind, quad):
        return pl.ds(pl.multiple_of(kind * features + quad * width, width), width)

    for slot in range(slots):
        at = slice(slot * positions, (slot + 1) * positions)
        length = lens_ref[0, 0, slot]
        allowed = causal & (key_ids < length)
        per_length = 1.0 / jnp.full((1, width), jnp.maximum(length, 1), jnp.int32).astype(F32)
        attended = []
        for quad in range(quads):
            query = proj[at, columns_of(2, quad)]
            keys = spread_heads(proj[at, columns_of(3, quad)])
            values = spread_heads(proj[at, columns_of(1, quad)])
            scores = dot(query, keys, 1, 1) * head ** (-0.5)
            gate = jax.nn.sigmoid(scores)
            weights = (jnp.where(allowed, scores * gate, 0.0) * per_length).astype(BF16)
            grade = jnp.where(allowed, gate * (1.0 + scores * (1.0 - gate)), 0.0)
            attended.append(dot(weights, values, 1, 0))
            kept_weights[at, columns_of(0, quad)] = weights
            kept_grades[at, columns_of(0, quad)] = grade * (per_length * head ** (-0.5))
        normal, scale = norm_parts(jnp.concatenate(attended, axis=1))
        grad = dgate[at, :].astype(F32)
        gates = proj[at, 0:features].astype(F32)
        dproj[at, 0:features] = (
            (grad * normal).astype(BF16).astype(F32) * slope[at, 0:features]
        ).astype(BF16)
        dgate[at, :] = norm_back(normal, scale, grad * gates).astype(BF16)

    def backward(quad):
        for slot in range(slots):
            at = slice(slot * positions, (slot + 1) * positions)
            query = proj[at, columns_of(2, quad)]
            keys = spread_heads(proj[at, columns_of(3, quad)])
            values = spread_heads(proj[at, columns_of(1, quad)])
            d_quad = dgate[at, columns_of(0, quad)]
            d_weights = dot(d_quad, values, 1, 1).astype(BF16).astype(F32)
            d_scores = (d_weights * kept_grades[at, columns_of(0, quad)]).astype(BF16)
            d_values = gather_heads(dot(kept_weights[at, columns_of(0, quad)], d_quad, 0, 0))
            d_query = dot(d_scores, keys, 1, 0)
            d_keys = gather_heads(dot(d_scores, query, 0, 0))
            for kind, value in ((1, d_values), (2, d_query), (3, d_keys)):
                columns = columns_of(kind, quad)
                dproj[at, columns] = (
                    value.astype(BF16).astype(F32) * slope[at, columns]
                ).astype(BF16)

    normed_t[...] = normed[...].T

    def grad_block(at):
        columns = slice(at * block, (at + 1) * block)
        dgate[:, columns] = dot(dproj[...], win[columns, :], 1, 1).astype(BF16)

    def finish(slot):
        at = slice(slot * positions, (slot + 1) * positions)
        grad = norm_back(*norm_parts(hist[slot].astype(F32)), dgate[at, :].astype(F32))
        return (cot[slot].astype(F32) + grad).astype(BF16)

    def product(columns):
        return dot(normed_t[...], dproj[:, columns], 1, 0).astype(BF16)

    return backward, product, [functools.partial(grad_block, i) for i in range(features // block)], finish


def local_scratch(slots, positions, features):
    rows = slots * positions
    return [
        pltpu.VMEM((slots, positions, features), BF16),
        pltpu.VMEM((slots, positions, features), BF16),
        pltpu.VMEM((features, 4 * features), BF16),
        pltpu.VMEM((features, features), BF16),
        pltpu.VMEM((rows, features), BF16),
        pltpu.VMEM((features, rows), BF16),
        pltpu.VMEM((rows, 4 * features), BF16),
        pltpu.VMEM((rows, 4 * features), F32),
        pltpu.VMEM((rows, features), BF16),
        pltpu.VMEM((rows, 4 * features), BF16),
        pltpu.VMEM((rows, features), BF16),
        pltpu.VMEM((rows, features), F32),
        pltpu.SemaphoreType.DMA((4,)),
    ]


def local_kernel(slots, positions, features, lens_ref, hist_hbm, cot_hbm, win_hbm, wout_hbm,
                 grad_ref, part_ref, *scratch):
    backward, product, grad_blocks, finish = local_body(
        slots, positions, features, lens_ref, hist_hbm.at[0, 0], cot_hbm.at[0, 0], win_hbm,
        wout_hbm, *scratch)
    for quad in range(HEADS // GROUP):
        backward(quad)
    block = 256
    for step in range(4 * features // block):
        columns = slice(step * block, (step + 1) * block)
        part_ref[:, columns] = product(columns)
    for grad_block in grad_blocks:
        grad_block()
    for slot in range(slots):
        grad_ref[0, 0, slot] = finish(slot)


def fused_kernel(slots, positions, features, groups, lens_ref, hist_hbm, cot_hbm, win_hbm,
                 wout_hbm, grad_ref, out_ref, *refs):
    split = len(local_scratch(slots, positions, features))
    scratch = refs[:split]
    (part, recv0, acc0, recv1, acc1, recv2, acc2, recv3,
     s0, r0, s1, r1, s2, r2, s3, r3) = refs[split:]
    features, width = part.shape[1:]
    tall = features // groups
    me, rep = lax.axis_index("seq"), lax.axis_index("rep")
    core = me % 2
    x_at = (me // 2) % 2
    y_at = me // 4
    a_at = x_at + core * (y_at - x_at)
    b_at = y_at + core * (x_at - y_at)
    a_step, b_step = 1 + core, 2 - core
    twin = me + 1 - 2 * core
    a_peer = me + 2 * a_step * (1 - 2 * a_at)
    b_peer = me + 2 * b_step * (1 - 2 * b_at)
    mirror, swap = 3 - rep, rep + 2 - 4 * (rep // 2)
    beside = rep + 1 - 2 * (rep % 2)
    reps = [mirror, swap, beside]
    barrier = pltpu.get_barrier_semaphore()
    for peer in (twin, a_peer, b_peer):
        pl.semaphore_signal(barrier, inc=1, device_id={"seq": peer}, device_id_type=MESH)
    for peer in reps:
        pl.semaphore_signal(barrier, inc=1, device_id={"rep": peer}, device_id_type=MESH)

    backward, product, grad_blocks, finish = local_body(
        slots, positions, features, lens_ref, hist_hbm.at[0, 0], cot_hbm.at[0, 0], win_hbm,
        wout_hbm, *scratch)
    pl.semaphore_wait(barrier, 3 + len(reps))

    def send(source, target, sent, got, peer):
        copy = pltpu.make_async_remote_copy(
            src_ref=source, dst_ref=target, send_sem=sent, recv_sem=got,
            device_id=peer, device_id_type=MESH,
        )
        copy.start()
        return copy

    def add(left, right):
        return (left.astype(F32) + right.astype(F32)).astype(BF16)

    def chip(a, b):
        return a * a_step + b * b_step

    order = ((1 - a_at, 1 - b_at), (1 - a_at, b_at), (a_at, 1 - b_at), (a_at, b_at))
    first, along, across, last = {}, {}, {}, {}

    def block_of(position, half):
        a, b = order[position]
        rank = 2 * chip(a, b) + half
        return product(pl.ds(pl.multiple_of(rank * width, width), width))

    strips = [pl.ds(pl.multiple_of(z * tall, tall), tall) for z in reps + [rep]]

    backward(1 - core)
    for i, j in enumerate((0, 2, 1, 3)):
        part[i] = block_of(j, 1 - core)
        first[i] = send(part.at[i], recv0.at[i], s0.at[i], r0.at[i], {"seq": twin})
    backward(core)
    for i in range(4):
        own = block_of(i, core)
        first[i].wait_recv()
        acc0[i] = add(own, recv0[i])
        if i < 2:
            for k, strip in enumerate(strips):
                along[i, k] = send(acc0.at[i, strip], recv1.at[i, k], s1.at[i, k],
                                   r1.at[i, k], {"seq": a_peer})

    def stage1(k):
        along[0, k].wait_recv()
        acc1[k] = add(acc0[2, strips[k]], recv1[0, k])
        across[k] = send(acc1.at[k], recv2.at[k], s2.at[k], r2.at[k], {"seq": b_peer})

    def stage2(k):
        along[1, k].wait_recv()
        across[k].wait_recv()
        total = acc0[3, strips[k]].astype(F32) + recv1[1, k].astype(F32) + recv2[k].astype(F32)
        if k < len(reps):
            acc2[k] = total.astype(BF16)
            last[k] = send(acc2.at[k], recv3.at[k], s3.at[k], r3.at[k], {"rep": reps[k]})
            return
        for d in range(len(reps)):
            last[d].wait_recv()
            total = total + recv3[d].astype(F32)
        out_ref[...] = total

    def store(slot):
        grad_ref[0, 0, slot] = finish(slot)

    fill = list(grad_blocks) + [functools.partial(store, slot) for slot in range(slots)]
    fill.pop(0)()
    for stage in (stage1, stage2):
        for k in range(len(strips)):
            stage(k)
            if fill:
                fill.pop(0)()
    for work in fill:
        work()
    for copies in (first, along, across, last):
        for copy in copies.values():
            copy.wait_send()


def leave_kernel(grad_in, total_in, grad_hbm, total_hbm, sems):
    copies = [pltpu.make_async_copy(total_in, total_hbm, sems.at[0]),
              pltpu.make_async_copy(grad_in, grad_hbm, sems.at[1])]
    for copy in copies:
        copy.start()
    for copy in copies:
        copy.wait()


def shards(histories, cotangents, lengths, w_in, w_out):
    slots, positions, features = histories.shape[2:]
    ranks, groups = lax.axis_size("seq"), lax.axis_size("rep")
    width = 4 * features // ranks
    tall = features // groups
    fast = ranks == 8 and groups == 4 and width % 128 == 0 and tall % 16 == 0 and width == GROUP * features // HEADS
    anywhere = pl.BlockSpec(memory_space=pl.ANY)
    inside = pl.BlockSpec(memory_space=pltpu.VMEM)
    in_specs = [pl.BlockSpec(memory_space=pltpu.SMEM)] + [pl.BlockSpec(memory_space=pltpu.HBM)] * 4
    grad_shape = jax.ShapeDtypeStruct(histories.shape, BF16)
    scratch = local_scratch(slots, positions, features)
    operands = (lengths, histories, cotangents, w_in, w_out)
    if not fast:
        grads, part = pl.pallas_call(
            functools.partial(local_kernel, slots, positions, features),
            out_shape=(grad_shape, jax.ShapeDtypeStruct((features, 4 * features), BF16)),
            in_specs=in_specs,
            out_specs=(inside, inside),
            scratch_shapes=scratch,
            name="local",
        )(*operands)
        column_block = lax.psum_scatter(part, "seq", scatter_dimension=1, tiled=True)
        total = lax.psum_scatter(column_block, "rep", scatter_dimension=0, tiled=True)
        return grads, total.astype(F32)
    shapes = [
        (4, features, width), (4, features, width), (4, features, width),
        (2, groups, tall, width), (groups, tall, width), (groups, tall, width),
        (groups - 1, tall, width), (groups - 1, tall, width),
    ]
    counts = [(4,), (2, groups), (groups,), (groups - 1,)]
    total_shape = jax.ShapeDtypeStruct((tall, width), F32)
    grads, total = pl.pallas_call(
        functools.partial(fused_kernel, slots, positions, features, groups),
        out_shape=(grad_shape, total_shape),
        in_specs=in_specs,
        out_specs=(inside, inside),
        scratch_shapes=scratch + [pltpu.VMEM(shape, BF16) for shape in shapes]
        + [pltpu.SemaphoreType.DMA(count) for count in counts for _ in range(2)],
        compiler_params=pltpu.CompilerParams(collective_id=0, has_side_effects=True,
                                             vmem_limit_bytes=32 * 1024 * 1024),
        name="fused",
    )(*operands)
    return pl.pallas_call(
        leave_kernel,
        out_shape=(grad_shape, total_shape),
        in_specs=[inside, inside],
        out_specs=(anywhere, anywhere),
        scratch_shapes=[pltpu.SemaphoreType.DMA((2,))],
        compiler_params=pltpu.CompilerParams(vmem_limit_bytes=4 * 1024 * 1024),
        name="leave",
    )(grads, total)


def solution(mesh):
    placed = (
        P("rep", "seq", None, None, None),
        P("rep", "seq", None, None, None),
        P("rep", "seq", None),
        P(),
        P(),
    )
    return jax.shard_map(
        shards,
        mesh=mesh,
        in_specs=placed,
        out_specs=(P("rep", "seq", None, None, None), P("rep", "seq")),
        check_vma=False,
    )
```

```python
import functools

import jax
import jax.numpy as jnp
from jax import lax
from jax.experimental import pallas as pl
from jax.experimental.pallas import tpu as pltpu
from jax.sharding import PartitionSpec as P

HEADS = 8
GROUP = 4
MESH = pl.DeviceIdType.MESH
F32 = jnp.float32
BF16 = jnp.bfloat16


def dot(left, right, left_dim, right_dim):
    return lax.dot_general(
        left, right, (((left_dim,), (right_dim,)), ((), ())), preferred_element_type=F32
    )


def norm_parts(values):
    average = jnp.mean(values, axis=-1, keepdims=True)
    centered = values - average
    spread = jnp.mean(centered * centered, axis=-1, keepdims=True)
    scale = lax.rsqrt(spread + 1e-06)
    return centered * scale, scale


def norm_back(normed, scale, cotangent):
    average = jnp.mean(cotangent, axis=-1, keepdims=True)
    along = jnp.mean(cotangent * normed, axis=-1, keepdims=True)
    return scale * (cotangent - average - normed * along)


def local_body(slots, positions, features, lens_ref, hist_hbm, cot_hbm, win_hbm, wout_hbm,
               hist, cot, win, wout, normed, normed_t, proj, slope, dgate,
               dproj, kept_weights, kept_grades, sems):
    rows = slots * positions
    head = features // HEADS
    width = GROUP * head
    quads = HEADS // GROUP
    block = 256
    copies = [
        pltpu.make_async_copy(hist_hbm, hist, sems.at[0]),
        pltpu.make_async_copy(cot_hbm, cot, sems.at[2]),
        pltpu.make_async_copy(wout_hbm, wout, sems.at[1]),
    ]

    def load(step):
        columns = pl.ds(pl.multiple_of(step * block, block), block)
        return pltpu.make_async_copy(win_hbm.at[:, columns], win.at[:, columns],
                                     sems.at[3 + step])

    copies[0].start()
    for step in range(4 * features // block):
        load(step).start()
    for copy in copies[1:]:
        copy.start()
    row_ids = lax.broadcasted_iota(jnp.int32, (positions, 1), 0)
    copies[0].wait()
    for slot in range(slots):
        part, _ = norm_parts(hist[slot].astype(F32))
        normed[slot * positions:(slot + 1) * positions, :] = part.astype(BF16)

    @pl.loop(0, 4 * features // block)
    def _(step):
        columns = pl.ds(pl.multiple_of(step * block, block), block)
        load(step).wait()
        out = dot(normed[...], win[:, columns], 1, 0)
        gate = jax.nn.sigmoid(out)
        proj[:, columns] = (out * gate).astype(BF16)
        slope[:, columns] = gate * (1.0 + out * (1.0 - gate))

    copies[1].wait()
    for slot in range(slots):
        valid = row_ids < lens_ref[0, 0, slot]
        cot[slot] = jnp.where(valid, cot[slot], jnp.zeros((), BF16))
    copies[2].wait()
    dgate[...] = dot(cot[...].reshape(rows, features), wout[...], 1, 1).astype(BF16)

    time_ids = lax.broadcasted_iota(jnp.int32, (positions, width), 0)
    key_ids = lax.broadcasted_iota(jnp.int32, (positions, width), 1) % positions
    causal = key_ids <= time_ids
    lane_head = lax.broadcasted_iota(jnp.int32, (positions, width), 1) // head

    def spread_heads(values):
        zero = jnp.zeros((), values.dtype)
        return jnp.concatenate(
            [jnp.where(lane_head == h, values, zero) for h in range(GROUP)], axis=0
        )

    def gather_heads(values):
        total = values[0:positions]
        for h in range(1, GROUP):
            total = jnp.where(lane_head == h, values[h * positions:(h + 1) * positions], total)
        return total

    def columns_of(kind, quad):
        return pl.ds(pl.multiple_of(kind * features + quad * width, width), width)

    for slot in range(slots):
        at = slice(slot * positions, (slot + 1) * positions)
        length = lens_ref[0, 0, slot]
        allowed = causal & (key_ids < length)
        per_length = 1.0 / jnp.full((1, width), jnp.maximum(length, 1), jnp.int32).astype(F32)
        attended = []
        for quad in range(quads):
            query = proj[at, columns_of(2, quad)]
            keys = spread_heads(proj[at, columns_of(3, quad)])
            values = spread_heads(proj[at, columns_of(1, quad)])
            scores = dot(query, keys, 1, 1) * head ** (-0.5)
            gate = jax.nn.sigmoid(scores)
            weights = (jnp.where(allowed, scores * gate, 0.0) * per_length).astype(BF16)
            grade = jnp.where(allowed, gate * (1.0 + scores * (1.0 - gate)), 0.0)
            attended.append(dot(weights, values, 1, 0))
            kept_weights[at, columns_of(0, quad)] = weights
            kept_grades[at, columns_of(0, quad)] = grade * (per_length * head ** (-0.5))
        normal, scale = norm_parts(jnp.concatenate(attended, axis=1))
        grad = dgate[at, :].astype(F32)
        gates = proj[at, 0:features].astype(F32)
        dproj[at, 0:features] = (
            (grad * normal).astype(BF16).astype(F32) * slope[at, 0:features]
        ).astype(BF16)
        dgate[at, :] = norm_back(normal, scale, grad * gates).astype(BF16)

    def backward(quad):
        for slot in range(slots):
            at = slice(slot * positions, (slot + 1) * positions)
            query = proj[at, columns_of(2, quad)]
            keys = spread_heads(proj[at, columns_of(3, quad)])
            values = spread_heads(proj[at, columns_of(1, quad)])
            d_quad = dgate[at, columns_of(0, quad)]
            d_weights = dot(d_quad, values, 1, 1).astype(BF16).astype(F32)
            d_scores = (d_weights * kept_grades[at, columns_of(0, quad)]).astype(BF16)
            d_values = gather_heads(dot(kept_weights[at, columns_of(0, quad)], d_quad, 0, 0))
            d_query = dot(d_scores, keys, 1, 0)
            d_keys = gather_heads(dot(d_scores, query, 0, 0))
            for kind, value in ((1, d_values), (2, d_query), (3, d_keys)):
                columns = columns_of(kind, quad)
                dproj[at, columns] = (
                    value.astype(BF16).astype(F32) * slope[at, columns]
                ).astype(BF16)

    normed_t[...] = normed[...].T

    def grad_block(at):
        columns = slice(at * block, (at + 1) * block)
        dgate[:, columns] = dot(dproj[...], win[columns, :], 1, 1).astype(BF16)

    def finish(slot):
        at = slice(slot * positions, (slot + 1) * positions)
        grad = norm_back(*norm_parts(hist[slot].astype(F32)), dgate[at, :].astype(F32))
        return (cot[slot].astype(F32) + grad).astype(BF16)

    def product(columns):
        return dot(normed_t[...], dproj[:, columns], 1, 0).astype(BF16)

    return backward, product, [functools.partial(grad_block, i) for i in range(features // block)], finish


def local_scratch(slots, positions, features):
    rows = slots * positions
    return [
        pltpu.VMEM((slots, positions, features), BF16),
        pltpu.VMEM((slots, positions, features), BF16),
        pltpu.VMEM((features, 4 * features), BF16),
        pltpu.VMEM((features, features), BF16),
        pltpu.VMEM((rows, features), BF16),
        pltpu.VMEM((features, rows), BF16),
        pltpu.VMEM((rows, 4 * features), BF16),
        pltpu.VMEM((rows, 4 * features), F32),
        pltpu.VMEM((rows, features), BF16),
        pltpu.VMEM((rows, 4 * features), BF16),
        pltpu.VMEM((rows, features), BF16),
        pltpu.VMEM((rows, features), F32),
        pltpu.SemaphoreType.DMA((3 + 4 * features // 256,)),
    ]


def local_kernel(slots, positions, features, lens_ref, hist_hbm, cot_hbm, win_hbm, wout_hbm,
                 grad_ref, part_ref, *scratch):
    backward, product, grad_blocks, finish = local_body(
        slots, positions, features, lens_ref, hist_hbm.at[0, 0], cot_hbm.at[0, 0], win_hbm,
        wout_hbm, *scratch)
    for quad in range(HEADS // GROUP):
        backward(quad)
    block = 256
    for step in range(4 * features // block):
        columns = slice(step * block, (step + 1) * block)
        part_ref[:, columns] = product(columns)
    for grad_block in grad_blocks:
        grad_block()
    for slot in range(slots):
        grad_ref[0, 0, slot] = finish(slot)


def fused_kernel(slots, positions, features, groups, lens_ref, hist_hbm, cot_hbm, win_hbm,
                 wout_hbm, grad_ref, out_ref, *refs):
    split = len(local_scratch(slots, positions, features))
    scratch = refs[:split]
    (part, recv0, acc0, recv1, acc1, recv2, acc2, recv3,
     s0, r0, s1, r1, s2, r2, s3, r3) = refs[split:]
    features, width = part.shape[1:]
    tall = features // groups
    me, rep = lax.axis_index("seq"), lax.axis_index("rep")
    core = me % 2
    x_at = (me // 2) % 2
    y_at = me // 4
    a_at = x_at + core * (y_at - x_at)
    b_at = y_at + core * (x_at - y_at)
    a_step, b_step = 1 + core, 2 - core
    twin = me + 1 - 2 * core
    a_peer = me + 2 * a_step * (1 - 2 * a_at)
    b_peer = me + 2 * b_step * (1 - 2 * b_at)
    mirror, swap = 3 - rep, rep + 2 - 4 * (rep // 2)
    beside = rep + 1 - 2 * (rep % 2)
    reps = [mirror, swap, beside]
    barrier = pltpu.get_barrier_semaphore()
    for peer in (twin, a_peer, b_peer):
        pl.semaphore_signal(barrier, inc=1, device_id={"seq": peer}, device_id_type=MESH)
    for peer in reps:
        pl.semaphore_signal(barrier, inc=1, device_id={"rep": peer}, device_id_type=MESH)

    backward, product, grad_blocks, finish = local_body(
        slots, positions, features, lens_ref, hist_hbm.at[0, 0], cot_hbm.at[0, 0], win_hbm,
        wout_hbm, *scratch)
    pl.semaphore_wait(barrier, 3 + len(reps))

    def send(source, target, sent, got, peer):
        copy = pltpu.make_async_remote_copy(
            src_ref=source, dst_ref=target, send_sem=sent, recv_sem=got,
            device_id=peer, device_id_type=MESH,
        )
        copy.start()
        return copy

    def add(left, right):
        return (left.astype(F32) + right.astype(F32)).astype(BF16)

    def chip(a, b):
        return a * a_step + b * b_step

    order = ((1 - a_at, 1 - b_at), (1 - a_at, b_at), (a_at, 1 - b_at), (a_at, b_at))
    first, along, across, last = {}, {}, {}, {}

    def block_of(position, half):
        a, b = order[position]
        rank = 2 * chip(a, b) + half
        return product(pl.ds(pl.multiple_of(rank * width, width), width))

    strips = [pl.ds(pl.multiple_of(z * tall, tall), tall) for z in reps + [rep]]

    backward(1 - core)
    for i, j in enumerate((0, 2, 1, 3)):
        part[i] = block_of(j, 1 - core)
        first[i] = send(part.at[i], recv0.at[i], s0.at[i], r0.at[i], {"seq": twin})
    backward(core)
    early = {0: ((0, 0), (0, 1)), 1: ((1, 0), (0, 2), (1, 1), (0, 3), (1, 2), (1, 3))}
    for i in range(4):
        own = block_of(i, core)
        first[i].wait_recv()
        acc0[i] = add(own, recv0[i])
        for j, k in early.get(i, ()):
            along[j, k] = send(acc0.at[j, strips[k]], recv1.at[j, k], s1.at[j, k],
                               r1.at[j, k], {"seq": a_peer})

    def stage1(k):
        along[0, k].wait_recv()
        acc1[k] = add(acc0[2, strips[k]], recv1[0, k])
        across[k] = send(acc1.at[k], recv2.at[k], s2.at[k], r2.at[k], {"seq": b_peer})

    def stage2(k):
        along[1, k].wait_recv()
        across[k].wait_recv()
        total = acc0[3, strips[k]].astype(F32) + recv1[1, k].astype(F32) + recv2[k].astype(F32)
        if k < len(reps):
            acc2[k] = total.astype(BF16)
            last[k] = send(acc2.at[k], recv3.at[k], s3.at[k], r3.at[k], {"rep": reps[k]})
            return
        for d in range(len(reps)):
            last[d].wait_recv()
            total = total + recv3[d].astype(F32)
        out_ref[...] = total

    def store(slot):
        grad_ref[0, 0, slot] = finish(slot)

    fill = list(grad_blocks) + [functools.partial(store, slot) for slot in range(slots)]
    stages = [None, (stage1, 0), (stage1, 1), (stage2, 0), (stage1, 2), (stage2, 1),
              (stage1, 3), (stage2, 2), None, (stage2, 3)]
    counts = [1, 1, 0, 1, 1, 1, 1, 1, slots, 0]
    for stage, count in zip(stages, counts):
        if stage:
            stage[0](stage[1])
        for work in fill[:count]:
            work()
        fill = fill[count:]
    for work in fill:
        work()
    for copies in (first, along, across, last):
        for copy in copies.values():
            copy.wait_send()


def leave_kernel(grad_in, total_in, grad_hbm, total_hbm, sems):
    copies = [pltpu.make_async_copy(total_in, total_hbm, sems.at[0]),
              pltpu.make_async_copy(grad_in, grad_hbm, sems.at[1])]
    for copy in copies:
        copy.start()
    for copy in copies:
        copy.wait()


def shards(histories, cotangents, lengths, w_in, w_out):
    slots, positions, features = histories.shape[2:]
    ranks, groups = lax.axis_size("seq"), lax.axis_size("rep")
    width = 4 * features // ranks
    tall = features // groups
    fast = ranks == 8 and groups == 4 and width % 128 == 0 and tall % 16 == 0 and width == GROUP * features // HEADS
    anywhere = pl.BlockSpec(memory_space=pl.ANY)
    inside = pl.BlockSpec(memory_space=pltpu.VMEM)
    in_specs = [pl.BlockSpec(memory_space=pltpu.SMEM)] + [pl.BlockSpec(memory_space=pltpu.HBM)] * 4
    grad_shape = jax.ShapeDtypeStruct(histories.shape, BF16)
    scratch = local_scratch(slots, positions, features)
    operands = (lengths, histories, cotangents, w_in, w_out)
    if not fast:
        grads, part = pl.pallas_call(
            functools.partial(local_kernel, slots, positions, features),
            out_shape=(grad_shape, jax.ShapeDtypeStruct((features, 4 * features), BF16)),
            in_specs=in_specs,
            out_specs=(inside, inside),
            scratch_shapes=scratch,
            name="local",
        )(*operands)
        column_block = lax.psum_scatter(part, "seq", scatter_dimension=1, tiled=True)
        total = lax.psum_scatter(column_block, "rep", scatter_dimension=0, tiled=True)
        return grads, total.astype(F32)
    shapes = [
        (4, features, width), (4, features, width), (4, features, width),
        (2, groups, tall, width), (groups, tall, width), (groups, tall, width),
        (groups - 1, tall, width), (groups - 1, tall, width),
    ]
    counts = [(4,), (2, groups), (groups,), (groups - 1,)]
    total_shape = jax.ShapeDtypeStruct((tall, width), F32)
    grads, total = pl.pallas_call(
        functools.partial(fused_kernel, slots, positions, features, groups),
        out_shape=(grad_shape, total_shape),
        in_specs=in_specs,
        out_specs=(inside, inside),
        scratch_shapes=scratch + [pltpu.VMEM(shape, BF16) for shape in shapes]
        + [pltpu.SemaphoreType.DMA(count) for count in counts for _ in range(2)],
        compiler_params=pltpu.CompilerParams(collective_id=0, has_side_effects=True,
                                             vmem_limit_bytes=55850000),
        name="fused",
    )(*operands)
    return pl.pallas_call(
        leave_kernel,
        out_shape=(grad_shape, total_shape),
        in_specs=[inside, inside],
        out_specs=(anywhere, anywhere),
        scratch_shapes=[pltpu.SemaphoreType.DMA((2,))],
        compiler_params=pltpu.CompilerParams(vmem_limit_bytes=4 * 1024 * 1024),
        name="leave",
    )(grads, total)


def solution(mesh):
    placed = (
        P("rep", "seq", None, None, None),
        P("rep", "seq", None, None, None),
        P("rep", "seq", None),
        P(),
        P(),
    )
    return jax.shard_map(
        shards,
        mesh=mesh,
        in_specs=placed,
        out_specs=(P("rep", "seq", None, None, None), P("rep", "seq")),
        check_vma=False,
    )
```

```python
import functools

import jax
import jax.numpy as jnp
from jax import lax
from jax.experimental import pallas as pl
from jax.experimental.pallas import tpu as pltpu
from jax.sharding import PartitionSpec as P

HEADS = 8
GROUP = 4
MESH = pl.DeviceIdType.MESH
F32 = jnp.float32
BF16 = jnp.bfloat16


def dot(left, right, left_dim, right_dim):
    return lax.dot_general(
        left, right, (((left_dim,), (right_dim,)), ((), ())), preferred_element_type=F32
    )


def norm_parts(values):
    average = jnp.mean(values, axis=-1, keepdims=True)
    centered = values - average
    spread = jnp.mean(centered * centered, axis=-1, keepdims=True)
    scale = lax.rsqrt(spread + 1e-06)
    return centered * scale, scale


def norm_back(normed, scale, cotangent):
    average = jnp.mean(cotangent, axis=-1, keepdims=True)
    along = jnp.mean(cotangent * normed, axis=-1, keepdims=True)
    return scale * (cotangent - average - normed * along)


def local_body(slots, positions, features, lens_ref, hist_hbm, cot_hbm, win_hbm, wout_hbm,
               hist, cot, win, wout, normed, normed_t, proj, slope, dgate,
               dproj, kept_weights, kept_grades, sems):
    rows = slots * positions
    head = features // HEADS
    width = GROUP * head
    quads = HEADS // GROUP
    block = 256
    copies = [
        pltpu.make_async_copy(hist_hbm, hist, sems.at[0]),
        pltpu.make_async_copy(cot_hbm, cot, sems.at[2]),
        pltpu.make_async_copy(wout_hbm, wout, sems.at[1]),
    ]

    def load(step):
        columns = pl.ds(pl.multiple_of(step * block, block), block)
        return pltpu.make_async_copy(win_hbm.at[:, columns], win.at[:, columns],
                                     sems.at[3 + step])

    copies[0].start()
    for step in range(4 * features // block):
        load(step).start()
    for copy in copies[1:]:
        copy.start()
    row_ids = lax.broadcasted_iota(jnp.int32, (positions, 1), 0)
    copies[0].wait()
    for slot in range(slots):
        part, _ = norm_parts(hist[slot].astype(F32))
        normed[slot * positions:(slot + 1) * positions, :] = part.astype(BF16)

    @pl.loop(0, 4 * features // block)
    def _(step):
        columns = pl.ds(pl.multiple_of(step * block, block), block)
        load(step).wait()
        out = dot(normed[...], win[:, columns], 1, 0)
        gate = jax.nn.sigmoid(out)
        proj[:, columns] = (out * gate).astype(BF16)
        slope[:, columns] = gate * (1.0 + out * (1.0 - gate))

    copies[1].wait()
    for slot in range(slots):
        valid = row_ids < lens_ref[0, 0, slot]
        cot[slot] = jnp.where(valid, cot[slot], jnp.zeros((), BF16))
    copies[2].wait()
    dgate[...] = dot(cot[...].reshape(rows, features), wout[...], 1, 1).astype(BF16)

    time_ids = lax.broadcasted_iota(jnp.int32, (positions, width), 0)
    key_ids = lax.broadcasted_iota(jnp.int32, (positions, width), 1) % positions
    causal = key_ids <= time_ids
    lane_head = lax.broadcasted_iota(jnp.int32, (positions, width), 1) // head

    def spread_heads(values):
        zero = jnp.zeros((), values.dtype)
        return jnp.concatenate(
            [jnp.where(lane_head == h, values, zero) for h in range(GROUP)], axis=0
        )

    def gather_heads(values):
        total = values[0:positions]
        for h in range(1, GROUP):
            total = jnp.where(lane_head == h, values[h * positions:(h + 1) * positions], total)
        return total

    def columns_of(kind, quad):
        return pl.ds(pl.multiple_of(kind * features + quad * width, width), width)

    for slot in range(slots):
        at = slice(slot * positions, (slot + 1) * positions)
        length = lens_ref[0, 0, slot]
        allowed = causal & (key_ids < length)
        per_length = 1.0 / jnp.full((1, width), jnp.maximum(length, 1), jnp.int32).astype(F32)
        attended = []
        for quad in range(quads):
            query = proj[at, columns_of(2, quad)]
            keys = spread_heads(proj[at, columns_of(3, quad)])
            values = spread_heads(proj[at, columns_of(1, quad)])
            scores = dot(query, keys, 1, 1) * head ** (-0.5)
            gate = jax.nn.sigmoid(scores)
            weights = (jnp.where(allowed, scores * gate, 0.0) * per_length).astype(BF16)
            grade = jnp.where(allowed, gate * (1.0 + scores * (1.0 - gate)), 0.0)
            attended.append(dot(weights, values, 1, 0))
            kept_weights[at, columns_of(0, quad)] = weights
            kept_grades[at, columns_of(0, quad)] = grade * (per_length * head ** (-0.5))
        normal, scale = norm_parts(jnp.concatenate(attended, axis=1))
        grad = dgate[at, :].astype(F32)
        gates = proj[at, 0:features].astype(F32)
        dproj[at, 0:features] = (
            (grad * normal).astype(BF16).astype(F32) * slope[at, 0:features]
        ).astype(BF16)
        dgate[at, :] = norm_back(normal, scale, grad * gates).astype(BF16)

    def backward(quad):
        for slot in range(slots):
            at = slice(slot * positions, (slot + 1) * positions)
            query = proj[at, columns_of(2, quad)]
            keys = spread_heads(proj[at, columns_of(3, quad)])
            values = spread_heads(proj[at, columns_of(1, quad)])
            d_quad = dgate[at, columns_of(0, quad)]
            d_weights = dot(d_quad, values, 1, 1).astype(BF16).astype(F32)
            d_scores = (d_weights * kept_grades[at, columns_of(0, quad)]).astype(BF16)
            d_values = gather_heads(dot(kept_weights[at, columns_of(0, quad)], d_quad, 0, 0))
            d_query = dot(d_scores, keys, 1, 0)
            d_keys = gather_heads(dot(d_scores, query, 0, 0))
            for kind, value in ((1, d_values), (2, d_query), (3, d_keys)):
                columns = columns_of(kind, quad)
                dproj[at, columns] = (
                    value.astype(BF16).astype(F32) * slope[at, columns]
                ).astype(BF16)

    normed_t[...] = normed[...].T

    def grad_block(at):
        columns = slice(at * block, (at + 1) * block)
        dgate[:, columns] = dot(dproj[...], win[columns, :], 1, 1).astype(BF16)

    def finish(slot):
        at = slice(slot * positions, (slot + 1) * positions)
        grad = norm_back(*norm_parts(hist[slot].astype(F32)), dgate[at, :].astype(F32))
        return (cot[slot].astype(F32) + grad).astype(BF16)

    def product(columns):
        return dot(normed_t[...], dproj[:, columns], 1, 0).astype(BF16)

    return backward, product, [functools.partial(grad_block, i) for i in range(features // block)], finish


def local_scratch(slots, positions, features):
    rows = slots * positions
    return [
        pltpu.VMEM((slots, positions, features), BF16),
        pltpu.VMEM((slots, positions, features), BF16),
        pltpu.VMEM((features, 4 * features), BF16),
        pltpu.VMEM((features, features), BF16),
        pltpu.VMEM((rows, features), BF16),
        pltpu.VMEM((features, rows), BF16),
        pltpu.VMEM((rows, 4 * features), BF16),
        pltpu.VMEM((rows, 4 * features), F32),
        pltpu.VMEM((rows, features), BF16),
        pltpu.VMEM((rows, 4 * features), BF16),
        pltpu.VMEM((rows, features), BF16),
        pltpu.VMEM((rows, features), F32),
        pltpu.SemaphoreType.DMA((3 + 4 * features // 256,)),
    ]


def local_kernel(slots, positions, features, lens_ref, hist_hbm, cot_hbm, win_hbm, wout_hbm,
                 grad_ref, part_ref, *scratch):
    backward, product, grad_blocks, finish = local_body(
        slots, positions, features, lens_ref, hist_hbm.at[0, 0], cot_hbm.at[0, 0], win_hbm,
        wout_hbm, *scratch)
    for quad in range(HEADS // GROUP):
        backward(quad)
    block = 256
    for step in range(4 * features // block):
        columns = slice(step * block, (step + 1) * block)
        part_ref[:, columns] = product(columns)
    for grad_block in grad_blocks:
        grad_block()
    for slot in range(slots):
        grad_ref[0, 0, slot] = finish(slot)


def fused_kernel(slots, positions, features, groups, lens_ref, hist_hbm, cot_hbm, win_hbm,
                 wout_hbm, grad_ref, out_ref, *refs):
    split = len(local_scratch(slots, positions, features))
    scratch = refs[:split]
    (part, recv0, acc0, recv1, acc1, recv2, acc2, recv3,
     s0, r0, s1, r1, s2, r2, s3, r3) = refs[split:]
    features, width = part.shape[1:]
    tall = features // groups
    me, rep = lax.axis_index("seq"), lax.axis_index("rep")
    core = me % 2
    x_at = (me // 2) % 2
    y_at = me // 4
    a_at = x_at + core * (y_at - x_at)
    b_at = y_at + core * (x_at - y_at)
    a_step, b_step = 1 + core, 2 - core
    twin = me + 1 - 2 * core
    a_peer = me + 2 * a_step * (1 - 2 * a_at)
    b_peer = me + 2 * b_step * (1 - 2 * b_at)
    mirror, swap = 3 - rep, rep + 2 - 4 * (rep // 2)
    beside = rep + 1 - 2 * (rep % 2)
    owners, reps = [mirror, beside, swap], [beside, beside, swap]
    barrier = pltpu.get_barrier_semaphore()
    for peer in (twin, a_peer, b_peer):
        pl.semaphore_signal(barrier, inc=1, device_id={"seq": peer}, device_id_type=MESH)
    for peer in (beside, swap):
        pl.semaphore_signal(barrier, inc=1, device_id={"rep": peer}, device_id_type=MESH)

    backward, product, grad_blocks, finish = local_body(
        slots, positions, features, lens_ref, hist_hbm.at[0, 0], cot_hbm.at[0, 0], win_hbm,
        wout_hbm, *scratch)
    pl.semaphore_wait(barrier, 5)

    def send(source, target, sent, got, peer):
        copy = pltpu.make_async_remote_copy(
            src_ref=source, dst_ref=target, send_sem=sent, recv_sem=got,
            device_id=peer, device_id_type=MESH,
        )
        copy.start()
        return copy

    def add(left, right):
        return (left.astype(F32) + right.astype(F32)).astype(BF16)

    def chip(a, b):
        return a * a_step + b * b_step

    order = ((1 - a_at, 1 - b_at), (1 - a_at, b_at), (a_at, 1 - b_at), (a_at, b_at))
    first, along, across, last = {}, {}, {}, {}

    def block_of(position, half):
        a, b = order[position]
        rank = 2 * chip(a, b) + half
        return product(pl.ds(pl.multiple_of(rank * width, width), width))

    strips = [pl.ds(pl.multiple_of(z * tall, tall), tall) for z in owners + [rep]]

    backward(1 - core)
    for i, j in enumerate((0, 2, 1, 3)):
        part[i] = block_of(j, 1 - core)
        first[i] = send(part.at[i], recv0.at[i], s0.at[i], r0.at[i], {"seq": twin})
    backward(core)
    early = {0: ((0, 0),), 1: ((1, 0), (0, 1), (1, 1), (0, 2), (1, 2), (0, 3), (1, 3))}
    for i in range(4):
        own = block_of(i, core)
        first[i].wait_recv()
        acc0[i] = add(own, recv0[i])
        for j, k in early.get(i, ()):
            along[j, k] = send(acc0.at[j, strips[k]], recv1.at[j, k], s1.at[j, k],
                               r1.at[j, k], {"seq": a_peer})

    def stage1(k):
        along[0, k].wait_recv()
        acc1[k] = add(acc0[2, strips[k]], recv1[0, k])
        across[k] = send(acc1.at[k], recv2.at[k], s2.at[k], r2.at[k], {"seq": b_peer})

    def stage2(k):
        along[1, k].wait_recv()
        across[k].wait_recv()
        total = acc0[3, strips[k]].astype(F32) + recv1[1, k].astype(F32) + recv2[k].astype(F32)
        if k == 2:
            last[0].wait_recv()
            total = total + recv3[0].astype(F32)
        if k < len(reps):
            acc2[k] = total.astype(BF16)
            last[k] = send(acc2.at[k], recv3.at[k], s3.at[k], r3.at[k], {"rep": reps[k]})
            return
        for d in (1, 2):
            last[d].wait_recv()
            total = total + recv3[d].astype(F32)
        out_ref[...] = total

    def store(slot):
        grad_ref[0, 0, slot] = finish(slot)

    fill = list(grad_blocks) + [functools.partial(store, slot) for slot in range(slots)]
    stages = [None, (stage1, 0), (stage1, 1), (stage2, 0), (stage1, 2), (stage2, 1),
              (stage1, 3), (stage2, 2), None, (stage2, 3)]
    counts = [1, 1, 0, 1, 1, 1, 1, 1, slots, 0]
    for stage, count in zip(stages, counts):
        if stage:
            stage[0](stage[1])
        for work in fill[:count]:
            work()
        fill = fill[count:]
    for work in fill:
        work()
    for copies in (first, along, across, last):
        for copy in copies.values():
            copy.wait_send()


def leave_kernel(grad_in, total_in, grad_hbm, total_hbm, sems):
    copies = [pltpu.make_async_copy(total_in, total_hbm, sems.at[0]),
              pltpu.make_async_copy(grad_in, grad_hbm, sems.at[1])]
    for copy in copies:
        copy.start()
    for copy in copies:
        copy.wait()


def shards(histories, cotangents, lengths, w_in, w_out):
    slots, positions, features = histories.shape[2:]
    ranks, groups = lax.axis_size("seq"), lax.axis_size("rep")
    width = 4 * features // ranks
    tall = features // groups
    fast = ranks == 8 and groups == 4 and width % 128 == 0 and tall % 16 == 0 and width == GROUP * features // HEADS
    anywhere = pl.BlockSpec(memory_space=pl.ANY)
    inside = pl.BlockSpec(memory_space=pltpu.VMEM)
    in_specs = [pl.BlockSpec(memory_space=pltpu.SMEM)] + [pl.BlockSpec(memory_space=pltpu.HBM)] * 4
    grad_shape = jax.ShapeDtypeStruct(histories.shape, BF16)
    scratch = local_scratch(slots, positions, features)
    operands = (lengths, histories, cotangents, w_in, w_out)
    if not fast:
        grads, part = pl.pallas_call(
            functools.partial(local_kernel, slots, positions, features),
            out_shape=(grad_shape, jax.ShapeDtypeStruct((features, 4 * features), BF16)),
            in_specs=in_specs,
            out_specs=(inside, inside),
            scratch_shapes=scratch,
            name="local",
        )(*operands)
        column_block = lax.psum_scatter(part, "seq", scatter_dimension=1, tiled=True)
        total = lax.psum_scatter(column_block, "rep", scatter_dimension=0, tiled=True)
        return grads, total.astype(F32)
    shapes = [
        (4, features, width), (4, features, width), (4, features, width),
        (2, groups, tall, width), (groups, tall, width), (groups, tall, width),
        (groups - 1, tall, width), (groups - 1, tall, width),
    ]
    counts = [(4,), (2, groups), (groups,), (groups - 1,)]
    total_shape = jax.ShapeDtypeStruct((tall, width), F32)
    grads, total = pl.pallas_call(
        functools.partial(fused_kernel, slots, positions, features, groups),
        out_shape=(grad_shape, total_shape),
        in_specs=in_specs,
        out_specs=(inside, inside),
        scratch_shapes=scratch + [pltpu.VMEM(shape, BF16) for shape in shapes]
        + [pltpu.SemaphoreType.DMA(count) for count in counts for _ in range(2)],
        compiler_params=pltpu.CompilerParams(collective_id=0, has_side_effects=True,
                                             vmem_limit_bytes=55850000),
        name="fused",
    )(*operands)
    return pl.pallas_call(
        leave_kernel,
        out_shape=(grad_shape, total_shape),
        in_specs=[inside, inside],
        out_specs=(anywhere, anywhere),
        scratch_shapes=[pltpu.SemaphoreType.DMA((2,))],
        compiler_params=pltpu.CompilerParams(vmem_limit_bytes=4 * 1024 * 1024),
        name="leave",
    )(grads, total)


def solution(mesh):
    placed = (
        P("rep", "seq", None, None, None),
        P("rep", "seq", None, None, None),
        P("rep", "seq", None),
        P(),
        P(),
    )
    return jax.shard_map(
        shards,
        mesh=mesh,
        in_specs=placed,
        out_specs=(P("rep", "seq", None, None, None), P("rep", "seq")),
        check_vma=False,
    )
```
